512 devices in a mesh: row: 32 (over x, z_lo), col: 16 (over z_hi, y, core).
Axes of the slice: x: 4, y: 4, z: 16 (z_hi: 2, z_lo: 8; z = z_hi * 8 + z_lo), core: 2. Of those that a mesh axis runs over, the one named last changes fastest.
Arguments:
- amplitudes: float32 [3072, 4, 2048], P(('row', 'col')), may hold values from -6 to 6
- integrals: float32 [8192, 4, 2048], P('row', None, 'col'), may hold values from -0.0625 to 0.0625
Outputs:
- ladder: float32 [3072, 8192], P('col', 'row')
The draws below stay inside these ranges and needn't reach their ends.
All inputs are finite; a program needn't handle non-finite values.
Results may differ from the reference program's by a relative error of at most 0.0001.
Values sent between devices are 32-bit elements; how exact they have to be, the bound alone decides.
No kernel may reach another device: no remote copies, remote signals or barrier semaphores. Data moves between devices by JAX's collectives and lax.ppermute only.
A program may use at most 64 MiB of HBM per device.

```python
import jax
import jax.numpy as jnp
from jax import lax

IJ = 3072
PANEL = 2048
PANELS = 4
AB = 8192


def steps_of(own_key, shape, shards, least, high):
    gain = 1.0
    for position, shards_of in shards:
        draws = jax.random.uniform(jax.random.fold_in(jax.random.fold_in(own_key, 6), position), (shards_of,), jnp.float32, least / len(shards), high / len(shards))
        gain = gain * jnp.repeat(jnp.exp(draws), shape[position] // shards_of).reshape((-1,) + (1,) * (len(shape) - 1 - position))
    return gain


def centred(own_key, extent, scale, most, cuts=(), held_as=jnp.bfloat16):
    drawn = jax.random.normal(own_key, extent, jnp.float32) * scale
    if len(cuts) > 0:
        drawn = steps_of(own_key, extent, cuts, -0.22, 0.18) * drawn
    return jnp.clip(drawn, min=-most, max=most).astype(held_as)


def setup_inputs(seed: int = 0) -> dict:
    streams_of = jax.random.split(jax.random.key(seed), 3)
    amplitudes = centred(streams_of[0], (IJ, PANELS, PANEL), 1.0, 6.0, ((0, 512),), jnp.float32)
    integrals = centred(streams_of[1], (AB, PANELS, PANEL), (PANEL * PANELS) ** -0.5, 0.0625, ((0, 32), (2, 16)), jnp.float32)
    return dict(amplitudes=amplitudes, integrals=integrals)


def reference(amplitudes, integrals):
    ladder = jnp.zeros((IJ, AB), jnp.float32)
    for panel in range(PANELS):
        panel_terms = jnp.dot(amplitudes[:, panel, :], integrals[:, panel, :].T, precision=lax.Precision.HIGHEST, preferred_element_type=jnp.float32)
        ladder = ladder + panel_terms
    return ladder
```

```python
import jax
import jax.numpy as jnp
from jax import lax
from jax.sharding import PartitionSpec as P


def per_device(amplitudes, integrals):
    width = integrals.shape[2]
    depth = amplitudes.shape[1] * width
    mixed = lax.all_to_all(amplitudes, "col", split_axis=2, concat_axis=0, tiled=True)
    mixed = mixed.reshape(mixed.shape[0], depth)
    weights = integrals.reshape(integrals.shape[0], depth)
    rows = lax.all_gather(mixed, "row", axis=0, tiled=True)
    total = lax.dot_general(
        rows,
        weights,
        (((1,), (1,)), ((), ())),
        precision=lax.Precision.HIGH,
        preferred_element_type=jnp.float32,
    )
    return lax.psum_scatter(total, "col", scatter_dimension=0, tiled=True)


def solution(mesh):
    in_specs = (P(("row", "col"), None, None), P("row", None, "col"))
    out_specs = P("col", "row")
    return jax.shard_map(
        per_device, mesh=mesh, in_specs=in_specs, out_specs=out_specs, check_vma=False
    )
```

```python
import jax
import jax.numpy as jnp
from jax import lax
from jax.sharding import Mesh
from jax.sharding import PartitionSpec as P

AXES = ("x", "s", "p", "zh", "y", "c")
SIZES = (4, 4, 2, 2, 4, 2)


def split(value):
    high = lax.reduce_precision(value, 8, 7)
    return high.astype(jnp.bfloat16), (value - high).astype(jnp.bfloat16)


def contract(rows, weights):
    return lax.dot_general(
        rows, weights, (((1,), (1,)), ((), ())), preferred_element_type=jnp.float32
    )


def shift(value, axis, by):
    size = lax.axis_size(axis)
    return lax.ppermute(value, axis, [((i + by) % size, i) for i in range(size)])


def rolled(value, by, axis):
    size = value.shape[axis]
    twice = jnp.concatenate([value, value], axis=axis)
    return lax.dynamic_slice_in_dim(twice, by, size, axis=axis)


def per_device(amplitudes, integrals):
    nx, ns, np_, nzh, ny, nc = SIZES
    rows, panels, _ = amplitudes.shape
    block, _, width = integrals.shape
    depth = panels * width
    x, p, c = (lax.axis_index(a) for a in ("x", "p", "c"))

    own = integrals.reshape(block, depth)
    pair = shift(own, "p", 1)
    weights = jnp.zeros((nx * np_, block, 3 * depth), jnp.bfloat16)
    for e, part in enumerate((own, pair)):
        for d in range(nx):
            piece = part
            if d:
                piece = shift(part, "x", d)
            place = np_ * ((x + d) % nx) + (p + e) % np_
            high, low = split(piece)
            piece = jnp.concatenate([high, low, high], axis=1)
            weights = lax.dynamic_update_slice_in_dim(weights, piece[None], place, 0)
    weights = weights.reshape(nx * np_ * block, 3 * depth)

    swap = [(a * ny + b, b * nx + a) for a in range(nx) for b in range(ny)]
    moved = lax.ppermute(amplitudes, ("x", "y"), swap)
    moved = moved.reshape(rows, panels, nzh, ny * nc, width).transpose(3, 2, 0, 1, 4)
    spread = lax.all_to_all(moved, ("y", "c"), 0, 0, tiled=True)
    spread = spread.transpose(1, 0, 2, 3, 4).reshape(nzh, 1, nx * nc * rows, depth)
    spread = jnp.broadcast_to(spread, (nzh, ns) + spread.shape[2:])
    spread = spread.reshape((nzh * ns,) + spread.shape[2:])
    held = lax.all_to_all(spread, ("zh", "s"), 0, 0, tiled=True)
    held = held.reshape(nzh, 2, 2, 2, 2, nc, rows, depth)
    held = held.transpose(2, 4, 1, 3, 0, 5, 6, 7)
    held = rolled(held, c, 0)
    group = nzh * nc * rows
    high, low = split(held.reshape(2, 8 * group, depth))
    held = jnp.concatenate([high, high, low], axis=2)

    away = contract(held[1], weights)
    home = contract(held[0], weights)
    home = home + shift(away, "c", 1)
    home = home.reshape(ny, 2 * group, home.shape[1])
    home = lax.all_to_all(home, "y", 0, 0, tiled=True)
    home = (home[0] + home[1]) + (home[2] + home[3])

    home = home.reshape(nzh, group, nx * np_, block).transpose(0, 2, 1, 3)
    home = home.reshape(nzh * nx * np_, group, block)
    out = lax.all_to_all(home, ("zh", "x", "p"), 0, 0, tiled=True)
    out = out.reshape(nzh, ny, np_, nzh, nc * rows, block)
    out = (out[0] + out[1]).transpose(1, 2, 0, 3, 4)
    return out.reshape(np_ * nzh * ny * nc * rows, block)


def solution(mesh):
    fine = Mesh(mesh.devices.reshape(SIZES), AXES)
    in_specs = (P(AXES, None, None), P(AXES[:3], None, AXES[3:]))
    out_specs = P(AXES[3:], AXES[:3])
    return jax.shard_map(
        per_device, mesh=fine, in_specs=in_specs, out_specs=out_specs, check_vma=False
    )
```

```python
import jax
import jax.numpy as jnp
from jax import lax
from jax.sharding import Mesh
from jax.sharding import PartitionSpec as P

AXES = ("x", "s", "p", "zh", "y", "c")
SIZES = (4, 4, 2, 2, 4, 2)


def split(value):
    high = lax.reduce_precision(value, 8, 7)
    return high.astype(jnp.bfloat16), (value - high).astype(jnp.bfloat16)


def contract(rows, weights):
    return lax.dot_general(
        rows, weights, (((1,), (1,)), ((), ())), preferred_element_type=jnp.float32
    )


def shift(value, axis, by):
    size = lax.axis_size(axis)
    return lax.ppermute(value, axis, [((i + by) % size, i) for i in range(size)])


def per_device(amplitudes, integrals):
    nx, ns, np_, nzh, ny, nc = SIZES
    rows, panels, _ = amplitudes.shape
    block, _, width = integrals.shape
    depth = panels * width
    x, p, c = (lax.axis_index(a) for a in ("x", "p", "c"))

    own = integrals.reshape(block, depth)
    pair = shift(own, "p", 1)
    pieces = {(0, 0): own, (1, 0): pair}
    for e, part in enumerate((own, pair)):
        for d in (1, nx - 1, 2):
            pieces[e, d] = shift(part, "x", d)
    swap = [(a * ny + b, b * nx + a) for a in range(nx) for b in range(ny)]
    moved = lax.ppermute(amplitudes, ("x", "y"), swap)
    moved, pieces[0, 0] = lax.optimization_barrier((moved, own))
    moved = moved.reshape(rows, panels, nzh, ny * nc, width).transpose(2, 3, 0, 1, 4)
    unit = rows * panels
    moved = moved.reshape(nzh, 1, ny * nc, unit, width)
    moved = jnp.broadcast_to(moved, (nzh, ns) + moved.shape[2:])
    moved = moved.reshape(nzh * ns * ny * nc, unit, width)
    held = lax.all_to_all(moved, ("zh", "s", "y", "c"), 0, 0, tiled=True)
    weights = None
    for (e, d), piece in pieces.items():
        place = np_ * ((x + d) & (nx - 1)) + (p ^ e)
        high, low = split(piece)
        piece = jnp.concatenate([high, low, high], axis=1)[None]
        if weights is None:
            weights = jnp.broadcast_to(piece, (nx * np_,) + piece.shape[1:])
        else:
            weights = lax.dynamic_update_slice_in_dim(weights, piece, place, 0)
    weights = weights.reshape(nx * np_ * block, 3 * depth)

    held = held.reshape(nzh, 2, 2, 2, 2, nc * unit, width)
    held = held.transpose(2, 4, 1, 3, 0, 5, 6).reshape(2, ny * nzh * nzh * nc * unit, width)
    group = nzh * nc * rows
    halves = []
    for index in (1 - c, c):
        half = lax.dynamic_index_in_dim(held, index, 0, keepdims=False)
        high, low = split(half.reshape(ny * nzh * group, depth))
        halves.append(jnp.concatenate([high, high, low], axis=1))

    away = contract(halves[0], weights)
    other = shift(away, "c", 1)
    home = lax.optimization_barrier(contract(halves[1], weights))
    home = home + other
    home = home.reshape(ny, nzh * group, home.shape[1])
    home = lax.all_to_all(home, "y", 0, 0, tiled=True)
    home = (home[0] + home[1]) + (home[2] + home[3])
    home = home.reshape(nzh, group, nx * np_, block).transpose(0, 2, 1, 3)
    home = home.reshape(nzh * nx * np_, group, block)
    out = lax.all_to_all(home, ("zh", "x", "p"), 0, 0, tiled=True)
    out = out.reshape(nzh, ny, np_, nzh, nc * rows, block)
    out = (out[0] + out[1]).transpose(1, 2, 0, 3, 4)
    return out.reshape(np_ * nzh * ny * nc * rows, block)


def solution(mesh):
    fine = Mesh(mesh.devices.reshape(SIZES), AXES)
    in_specs = (P(AXES, None, None), P(AXES[:3], None, AXES[3:]))
    out_specs = P(AXES[3:], AXES[:3])
    return jax.shard_map(
        per_device, mesh=fine, in_specs=in_specs, out_specs=out_specs, check_vma=False
    )
```

```python
import jax
import jax.numpy as jnp
from jax import lax
from jax.sharding import Mesh
from jax.sharding import PartitionSpec as P

AXES = ("x", "s", "p", "zh", "y", "c")
SIZES = (4, 4, 2, 2, 4, 2)


def split(value):
    high = lax.reduce_precision(value, 8, 7)
    return high.astype(jnp.bfloat16), (value - high).astype(jnp.bfloat16)


def contract(rows, weights):
    return lax.dot_general(
        rows, weights, (((1,), (1,)), ((), ())), preferred_element_type=jnp.float32
    )


def shift(value, axis, by):
    size = lax.axis_size(axis)
    return lax.ppermute(value, axis, [((i + by) % size, i) for i in range(size)])


def per_device(amplitudes, integrals):
    nx, ns, np_, nzh, ny, nc = SIZES
    rows, panels, _ = amplitudes.shape
    block, _, width = integrals.shape
    depth = panels * width
    x, p, c = (lax.axis_index(a) for a in ("x", "p", "c"))

    own = integrals.reshape(block, depth)
    pair = shift(own, "p", 1)
    pieces = {(0, 0): own, (1, 0): pair}
    for e, part in enumerate((own, pair)):
        for d in (1, nx - 1, 2):
            pieces[e, d] = shift(part, "x", d)
    swap = [(a * ny + b, b * nx + a) for a in range(nx) for b in range(ny)]
    moved = lax.ppermute(amplitudes, ("x", "y"), swap)
    moved, pieces[0, 0] = lax.optimization_barrier((moved, own))
    moved = moved.reshape(rows, panels, nzh, ny * nc, width).transpose(3, 2, 0, 1, 4)
    unit = rows * panels
    moved = moved.reshape(ny * nc, 1, nzh, unit, width)
    moved = jnp.broadcast_to(moved, (ny * nc, ns, nzh, unit, width))
    moved = moved.reshape(ny * nc * ns * nzh, unit, width)
    held = lax.all_to_all(moved, ("y", "c", "s", "zh"), 0, 0, tiled=True)
    weights = None
    for (e, d), piece in pieces.items():
        place = np_ * ((x + d) & (nx - 1)) + (p ^ e)
        high, low = split(piece)
        piece = jnp.concatenate([high, low, high], axis=1)[None]
        if weights is None:
            weights = jnp.broadcast_to(piece, (nx * np_,) + piece.shape[1:])
        else:
            weights = lax.dynamic_update_slice_in_dim(weights, piece, place, 0)
    weights = weights.reshape(nx * np_ * block, 3 * depth)

    held = held.reshape(2, 2, nc, 2, 2, nzh, unit, width)
    held = held.transpose(4, 1, 3, 0, 5, 2, 6, 7)
    held = held.reshape(2, ny * nzh * nzh * nc * unit, width)
    group = nzh * nc * rows
    halves = []
    for index in (1 - c, c):
        half = lax.dynamic_index_in_dim(held, index, 0, keepdims=False)
        high, low = split(half.reshape(ny * nzh * group, depth))
        halves.append(jnp.concatenate([high, high, low], axis=1))

    away = contract(halves[0], weights)
    other = shift(away, "c", 1)
    home = lax.optimization_barrier(contract(halves[1], weights))
    home = home + other
    home = home.reshape(ny, nzh * group, home.shape[1])
    home = lax.all_to_all(home, "y", 0, 0, tiled=True)
    home = (home[0] + home[1]) + (home[2] + home[3])
    home = home.reshape(nzh, group, nx * np_, block).transpose(2, 0, 1, 3)
    home = home.reshape(nx * np_ * nzh, group, block)
    out = lax.all_to_all(home, ("x", "p", "zh"), 0, 0, tiled=True)
    out = out.reshape(ny, np_, nzh, nzh, nc * rows, block)
    out = (out[:, :, 0] + out[:, :, 1]).transpose(1, 2, 0, 3, 4)
    return out.reshape(np_ * nzh * ny * nc * rows, block)


def solution(mesh):
    fine = Mesh(mesh.devices.reshape(SIZES), AXES)
    in_specs = (P(AXES, None, None), P(AXES[:3], None, AXES[3:]))
    out_specs = P(AXES[3:], AXES[:3])
    return jax.shard_map(
        per_device, mesh=fine, in_specs=in_specs, out_specs=out_specs, check_vma=False
    )
```

```python
import jax
import jax.numpy as jnp
from jax import lax
from jax.sharding import Mesh
from jax.sharding import PartitionSpec as P

AXES = ("x", "s", "p", "zh", "y", "c")
SIZES = (4, 4, 2, 2, 4, 2)


def split(value):
    high = lax.reduce_precision(value, 8, 7)
    return high.astype(jnp.bfloat16), (value - high).astype(jnp.bfloat16)


def contract(rows, weights):
    return lax.dot_general(
        rows, weights, (((1,), (1,)), ((), ())), preferred_element_type=jnp.float32
    )


def shift(value, axis, by):
    size = lax.axis_size(axis)
    return lax.ppermute(value, axis, [((i + by) % size, i) for i in range(size)])


def per_device(amplitudes, integrals):
    nx, ns, np_, nzh, ny, nc = SIZES
    rows, panels, _ = amplitudes.shape
    block, _, width = integrals.shape
    depth = panels * width
    x, p, c = (lax.axis_index(a) for a in ("x", "p", "c"))

    own = integrals.reshape(block, depth)
    pair = shift(own, "p", 1)
    pieces = {(0, 0): own, (1, 0): pair}
    for e, part in enumerate((own, pair)):
        for d in (1, nx - 1):
            pieces[e, d] = shift(part, "x", d)
        low = shift(pieces[e, 1][: block // 2], "x", 1)
        high = shift(pieces[e, nx - 1][block // 2 :], "x", nx - 1)
        pieces[e, 2] = jnp.concatenate([low, high], axis=0)
    swap = [(a * ny + b, b * nx + a) for a in range(nx) for b in range(ny)]
    moved = lax.ppermute(amplitudes, ("x", "y"), swap)
    moved, pieces[0, 0] = lax.optimization_barrier((moved, own))
    moved = moved.reshape(rows, panels, nzh, ny * nc, width).transpose(3, 2, 0, 1, 4)
    unit = rows * panels
    moved = moved.reshape(ny * nc, 1, nzh, unit, width)
    moved = jnp.broadcast_to(moved, (ny * nc, ns, nzh, unit, width))
    moved = moved.reshape(ny * nc * ns * nzh, unit, width)
    held = lax.all_to_all(moved, ("y", "c", "s", "zh"), 0, 0, tiled=True)
    weights = None
    for (e, d), piece in pieces.items():
        place = np_ * ((x + d) & (nx - 1)) + (p ^ e)
        high, low = split(piece)
        piece = jnp.concatenate([high, low, high], axis=1)[None]
        if weights is None:
            weights = jnp.broadcast_to(piece, (nx * np_,) + piece.shape[1:])
        else:
            weights = lax.dynamic_update_slice_in_dim(weights, piece, place, 0)
    weights = weights.reshape(nx * np_ * block, 3 * depth)

    held = held.reshape(2, 2, nc, 2, 2, nzh, unit, width)
    held = held.transpose(4, 1, 3, 0, 5, 2, 6, 7)
    held = held.reshape(2, ny * nzh * nzh * nc * unit, width)
    group = nzh * nc * rows
    halves = []
    for index in (1 - c, c):
        half = lax.dynamic_index_in_dim(held, index, 0, keepdims=False)
        high, low = split(half.reshape(ny * nzh * group, depth))
        halves.append(jnp.concatenate([high, high, low], axis=1))

    away = contract(halves[0], weights)
    other = shift(away, "c", 1)
    home = lax.optimization_barrier(contract(halves[1], weights))
    home = home + other
    home = home.reshape(ny, nzh * group, home.shape[1])
    home = lax.all_to_all(home, "y", 0, 0, tiled=True)
    home = (home[0] + home[1]) + (home[2] + home[3])
    home = home.reshape(nzh, group, nx * np_, block).transpose(2, 0, 1, 3)
    home = home.reshape(nx * np_ * nzh, group, block)
    out = lax.all_to_all(home, ("x", "p", "zh"), 0, 0, tiled=True)
    out = out.reshape(ny, np_, nzh, nzh, nc * rows, block)
    out = (out[:, :, 0] + out[:, :, 1]).transpose(1, 2, 0, 3, 4)
    return out.reshape(np_ * nzh * ny * nc * rows, block)


def solution(mesh):
    fine = Mesh(mesh.devices.reshape(SIZES), AXES)
    in_specs = (P(AXES, None, None), P(AXES[:3], None, AXES[3:]))
    out_specs = P(AXES[3:], AXES[:3])
    return jax.shard_map(
        per_device, mesh=fine, in_specs=in_specs, out_specs=out_specs, check_vma=False
    )
```
